32 devices in a mesh: seq: 8 (over z, y), head: 4 (over x, core).
Axes of the slice: x: 2, y: 2, z: 4, core: 2. Of those that a mesh axis runs over, the one named last changes fastest.
Arguments:
- tokens: bfloat16 [4096, 2048], P(('seq', 'head')), may hold values from -6 to 6
- w_in_x: bfloat16 [2048, 4096], P(None, 'head'), may hold values from -0.125 to 0.125
- w_in_z: bfloat16 [2048, 4096], P(None, 'head'), may hold values from -0.125 to 0.125
- w_in_bc: bfloat16 [2048, 256], replicated, may hold values from -0.125 to 0.125
- w_dt: bfloat16 [2048, 64], P(None, 'head'), may hold values from -0.125 to 0.125
- conv_x: float32 [4, 4096], P(None, 'head'), may hold values from -3 to 3
- conv_bc: float32 [4, 256], replicated, may hold values from -3 to 3
- dt_bias: float32 [64], P('head'), may hold values from -1 to 1
- decay_rate: float32 [64], P('head'), may hold values from 1.2207031e-05 to 0.05, as said below
- skip: float32 [64], P('head'), may hold values from 0.5 to 1.5
- norm_gain: float32 [4096], P('head'), may hold values from 0.25 to 1.75
- w_out: bfloat16 [4096, 2048], P('head'), may hold values from -0.09375 to 0.09375
Outputs:
- mixed: bfloat16 [4096, 2048], P(('seq', 'head'))
The draws below stay inside these ranges and needn't reach their ends.
Inputs may be any that keep to these rules, and one draw needn't show every extreme that they name: `decay_rate`: positive per-head decay rates.
All inputs are finite; a program needn't handle non-finite values.
Results may differ from the reference program's by a relative error of at most 0.013.
Values may be sent and summed in bfloat16 or wider, within the bound.
A program may use at most 128 MiB of HBM per device.

```python
import math
import jax
import jax.numpy as jnp
from jax import lax

D = 2048
H = 64
HEADDIM = 64
STATE = 128
SPAN = 256
KERNEL = 4
E = 4096
TOKENS = 4096
N_HEAD = 4


def draw_decay_rate(key, part):
    lowest = 0.05 / TOKENS
    return jnp.exp(jax.random.uniform(jax.random.fold_in(key, 14), (H,), minval=math.log(lowest), maxval=math.log(0.05))).astype(jnp.float32)


def shard_levels(own_key, extent, cuts, least, largest):
    gain = 1.0
    for dim, blocks in cuts:
        steps = jax.random.uniform(jax.random.fold_in(jax.random.fold_in(own_key, 6), dim), (blocks,), jnp.float32, least / len(cuts), largest / len(cuts))
        gain = gain * jnp.repeat(jnp.exp(steps), extent[dim] // blocks).reshape((-1,) + (1,) * (len(extent) - 1 - dim))
    return gain


def bell_draw(own_key, dims, scale, limit, cuts=(), kind=jnp.bfloat16):
    entries = jax.random.normal(own_key, dims, jnp.float32) * scale
    if len(cuts) > 0:
        entries = shard_levels(own_key, dims, cuts, -0.22, 0.18) * entries
    return jnp.clip(entries, min=-limit, max=limit).astype(kind)


def setup_inputs(seed: int = 0) -> dict:
    key_list = jax.random.split(jax.random.key(seed), 13)
    return {
        "tokens": bell_draw(key_list[0], (TOKENS, D), 1.0, 6.0, ((0, 32),)),
        "w_in_x": bell_draw(key_list[1], (D, E), D ** -0.5, 0.125, ((1, 4),)),
        "w_in_z": bell_draw(key_list[2], (D, E), D ** -0.5, 0.125, ((1, 4),)),
        "w_in_bc": bell_draw(key_list[3], (D, 2 * STATE), D ** -0.5, 0.125),
        "w_dt": bell_draw(key_list[4], (D, H), D ** -0.5, 0.125, ((1, 4),)),
        "conv_x": bell_draw(key_list[5], (KERNEL, E), KERNEL ** -0.5, 3.0, ((1, 4),), jnp.float32),
        "conv_bc": bell_draw(key_list[6], (KERNEL, 2 * STATE), KERNEL ** -0.5, 3.0, (), jnp.float32),
        "dt_bias": jnp.clip(jax.random.uniform(key_list[7], (H,), jnp.float32, -1.0, 1.0) * shard_levels(key_list[7], (H,), ((0, 4),), -0.4, 0.0), -1.0, 1.0),
        "decay_rate": draw_decay_rate(jax.random.fold_in(key_list[12], 71), 0),
        "skip": jnp.clip(0.5 + 1.0 * jax.random.uniform(key_list[9], (H,), jnp.float32) ** shard_levels(key_list[9], (H,), ((0, 4),), -0.2, 0.2), 0.5, 1.5),
        "norm_gain": jnp.clip(1.0 + 0.15 * jax.random.normal(key_list[10], (E,), jnp.float32), 0.25, 1.75),
        "w_out": bell_draw(key_list[11], (E, D), E ** -0.5, 0.09375, ((0, 4),)),
    }


highest = lax.Precision.HIGHEST

def span_update(state, x_span, step_span, decay_span, b_span, c_span, skip):
    cumul = jnp.cumsum(decay_span, axis=0)
    length = x_span.shape[0]
    lower = jnp.arange(length)[:, None] >= jnp.arange(length)[None, :]
    spread = cumul.T[:, :, None] - cumul.T[:, None, :]
    within = jnp.exp(jnp.where(lower[None], spread, -jnp.inf))
    scores = jnp.dot(c_span, b_span.T, precision=highest)
    scaled = x_span * step_span[:, :, None]
    output = jnp.einsum('hts,shp->thp', within * scores[None], scaled, precision=highest)
    output = output + jnp.einsum('tn,hpn->thp', c_span, state, precision=highest) * jnp.exp(cumul)[:, :, None]
    output = output + skip[None, :, None] * x_span
    remain = jnp.exp(cumul[-1][None, :] - cumul)
    fresh = jnp.einsum('shp,sn->hpn', scaled * remain[:, :, None], b_span, precision=highest)
    return (jnp.exp(cumul[-1])[:, None, None] * state + fresh, output, cumul)

def causal_conv(values, before, kernel):
    padded = jnp.concatenate([before, values], axis=0)
    length = values.shape[0]
    result = kernel[0] * padded[0:length]
    for offset in range(1, kernel.shape[0]):
        result = result + kernel[offset] * padded[offset:offset + length]
    return jax.nn.silu(result)

def reference(tokens, w_in_x, w_in_z, w_in_bc, w_dt, conv_x, conv_bc, dt_bias, decay_rate, skip, norm_gain, w_out):
    x_proj = jnp.dot(tokens, w_in_x, preferred_element_type=jnp.float32)
    gate_proj = jnp.dot(tokens, w_in_z, preferred_element_type=jnp.float32)
    bc_proj = jnp.dot(tokens, w_in_bc, preferred_element_type=jnp.float32)
    step_raw = jnp.dot(tokens, w_dt, preferred_element_type=jnp.float32)
    x_conv = causal_conv(x_proj, jnp.zeros((KERNEL - 1, x_proj.shape[1]), jnp.float32), conv_x)
    bc_conv = causal_conv(bc_proj, jnp.zeros((KERNEL - 1, bc_proj.shape[1]), jnp.float32), conv_bc)
    step_size = jax.nn.softplus(step_raw + dt_bias)
    log_decay = -step_size * decay_rate
    spans = TOKENS // SPAN

    def advance(state, inputs):
        x_span, step_span, decay_span, bc_span = inputs
        state, output, cumul = span_update(state, x_span, step_span, decay_span, bc_span[:, :STATE], bc_span[:, STATE:], skip)
        return (state, output)
    initial = jnp.zeros((H, HEADDIM, STATE), jnp.float32)
    final_state, outputs = lax.scan(advance, initial, (x_conv.reshape(spans, SPAN, H, HEADDIM), step_size.reshape(spans, SPAN, H), log_decay.reshape(spans, SPAN, H), bc_conv.reshape(spans, SPAN, 2 * STATE)))
    ssd_out = outputs.reshape(TOKENS, E)
    gated = ssd_out * jax.nn.silu(gate_proj)
    meansq = lax.optimization_barrier(jnp.mean(gated * gated, axis=1))
    normed = (gated * lax.rsqrt(meansq + 1e-05)[:, None] * norm_gain).astype(jnp.bfloat16)
    share = E // N_HEAD
    summed = jnp.zeros((TOKENS, D), jnp.float32)
    for member in range(N_HEAD):
        partial_term = jnp.dot(normed[:, member * share:(member + 1) * share], w_out[member * share:(member + 1) * share], preferred_element_type=jnp.float32).astype(jnp.bfloat16)
        summed = summed + lax.optimization_barrier(partial_term).astype(jnp.float32)
    return summed.astype(jnp.bfloat16)
```

```python
import functools
import jax
import jax.numpy as jnp
from jax import lax
from jax.experimental import pallas as pl
from jax.experimental.pallas import tpu as pltpu
from jax.sharding import PartitionSpec as P

CHUNK = 128
KERNEL = 4
F32 = jnp.float32
BF16 = jnp.bfloat16
highest = lax.Precision.HIGHEST


def passed_along(block, axis, distance):
    devices = range(lax.axis_size(axis))
    route = [(i - distance, i) for i in devices if i - distance in devices]
    return lax.ppermute(block, axis, route)


def widen(columns, width):
    rows, heads = columns.shape
    lane = lax.broadcasted_iota(jnp.int32, (rows, 2 * width), 1)
    parts = []
    for h in range(0, heads, 2):
        left = jnp.broadcast_to(columns[:, h : h + 1], (rows, 2 * width))
        right = jnp.broadcast_to(columns[:, h + 1 : h + 2], (rows, 2 * width))
        parts.append(jnp.where(lane < width, left, right))
    return jnp.concatenate(parts, axis=1)


def conv_state_kernel(width, x_ref, before_ref, taps_ref, weight_ref, total_ref, b_ref, conv_ref, state_ref, pad_ref):
    rows = x_ref.shape[0]
    pad_ref[0:8, :] = before_ref[...]
    pad_ref[8 : 8 + rows, :] = x_ref[...]
    for r in range(0, rows, CHUNK):
        acc = taps_ref[0:1, :] * pad_ref[r + 5 : r + 5 + CHUNK, :]
        for k in range(1, KERNEL):
            acc = acc + taps_ref[k : k + 1, :] * pad_ref[r + 5 + k : r + 5 + k + CHUNK, :]
        value = acc / (1.0 + jnp.exp(-acc))
        conv_ref[r : r + CHUNK, :] = value
        fresh = (value * widen(weight_ref[0, r : r + CHUNK, :], width)).astype(BF16)
        part = lax.dot_general(
            b_ref[r : r + CHUNK, :], fresh, (((0,), (0,)), ((), ())), preferred_element_type=F32
        )
        state = part if r == 0 else state + part
    n = state.shape[0]
    state_ref[0:n, :] = state.astype(BF16)
    decay = jnp.broadcast_to(jnp.exp(total_ref[0]), (16, total_ref.shape[2]))
    state_ref[n : n + 16, :] = widen(decay, width).astype(BF16)


def local_kernel(width, x_ref, step_ref, cum_ref, cumt_ref, b_ref, c_ref, skip_ref, y_ref):
    rows, cols = x_ref.shape
    heads = cols // width
    t = lax.broadcasted_iota(jnp.int32, (CHUNK, CHUNK), 0)
    s = lax.broadcasted_iota(jnp.int32, (CHUNK, CHUNK), 1)
    lower = t >= s
    lane = lax.broadcasted_iota(jnp.int32, (CHUNK, 2 * width), 1)
    skip = widen(jnp.broadcast_to(skip_ref[0], (8, heads)), width)[0:1, :]
    state = None
    base = jnp.zeros((1, heads), F32)
    for r in range(0, rows, CHUNK):
        x = x_ref[r : r + CHUNK, :]
        b = b_ref[r : r + CHUNK, :]
        c = c_ref[r : r + CHUNK, :]
        cum = cum_ref[0, r : r + CHUNK, :]
        scaled = x * widen(step_ref[0, r : r + CHUNK, :], width)
        narrow = scaled.astype(BF16)
        scores = lax.dot_general(c, b, (((1,), (1,)), ((), ())), preferred_element_type=F32)
        scores = jnp.where(lower, scores, 0.0)
        pieces = []
        for h in range(0, heads, 2):
            pair = narrow[:, h * width : (h + 2) * width]
            both = []
            for g in (h, h + 1):
                spread = cum[:, g : g + 1] - cumt_ref[0, g : g + 1, r : r + CHUNK]
                within = scores * jnp.exp(jnp.minimum(spread, 0.0))
                both.append(jnp.dot(within.astype(BF16), pair, preferred_element_type=F32))
            pieces.append(jnp.where(lane < width, both[0], both[1]))
        y = jnp.concatenate(pieces, axis=1) + skip * x
        last = cum_ref[0, r + CHUNK - 1 : r + CHUNK, :]
        if state is not None:
            y = y + jnp.dot(c, state.astype(BF16), preferred_element_type=F32) * widen(
                jnp.exp(cum - base), width
            )
        y_ref[r : r + CHUNK, :] = y
        if r + CHUNK < rows:
            rest = (scaled * widen(jnp.exp(last - cum), width)).astype(BF16)
            fresh = lax.dot_general(b, rest, (((0,), (0,)), ((), ())), preferred_element_type=F32)
            if state is None:
                state = fresh
            else:
                kept = widen(jnp.broadcast_to(jnp.exp(last - base), (8, heads)), width)[0:1, :]
                state = kept * state + fresh
            base = last


def gate_kernel(width, y_ref, z_ref, grow_ref, c_ref, state_ref, gain_ref, out_ref, sq_ref):
    j = pl.program_id(0)

    @pl.when(j == 0)
    def _():
        sq_ref[...] = jnp.zeros_like(sq_ref)

    for r in range(0, y_ref.shape[0], CHUNK):
        at = slice(r, r + CHUNK)
        carried = jnp.dot(c_ref[at, :], state_ref[...], preferred_element_type=F32)
        ssd = y_ref[at, :] + carried * widen(grow_ref[0, at, :], width)
        z = z_ref[at, :]
        gated = ssd * (z / (1.0 + jnp.exp(-z)))
        sq_ref[at, :] += jnp.sum(gated * gated, axis=1, keepdims=True)
        out_ref[at, :] = (gated * gain_ref[...]).astype(BF16)


def per_device(
    tokens, w_in_x, w_in_z, w_in_bc, w_dt, conv_x, conv_bc, dt_bias, decay_rate, skip, norm_gain, w_out
):
    cols = w_in_x.shape[1]
    heads = dt_bias.shape[0]
    width = cols // heads
    n = w_in_bc.shape[1] // 2
    inner = cols * lax.axis_size("head")
    rows_all = lax.all_gather(tokens, "head", axis=0, tiled=True)
    rows = rows_all.shape[0]
    dot = functools.partial(jnp.dot, preferred_element_type=F32)
    x_proj = dot(rows_all, w_in_x)
    small = dot(rows_all, jnp.concatenate([w_in_bc, w_dt], axis=1))
    bc_proj, step_raw = small[:, : 2 * n], small[:, 2 * n :]
    before = passed_along(
        jnp.concatenate([x_proj[-8:], bc_proj[-8:]], axis=1), "seq", 1
    )
    x_before, bc_before = before[:, :cols], before[:, cols:]
    padded = jnp.concatenate([bc_before, bc_proj], axis=0)
    bc = sum(conv_bc[k] * padded[5 + k : 5 + k + rows] for k in range(KERNEL))
    bc = jax.nn.silu(bc).astype(BF16)
    b_mat, c_mat = bc[:, :n], bc[:, n:]
    step = jax.nn.softplus(step_raw + dt_bias)
    order = jnp.arange(rows)
    tri = (order[:, None] >= order[None, :]).astype(F32)
    cumul = jnp.dot(tri, -step * decay_rate, precision=highest)
    total = cumul[-1:]

    hb = min(heads, 256 // width)
    blocks = heads // hb
    wide = hb * width

    def by_block(a):
        return a.reshape(a.shape[0], blocks, hb).transpose(1, 0, 2)

    total3 = by_block(total)
    full = lambda r: pl.BlockSpec((r, wide), lambda j: (0, j))
    same = lambda r, c: pl.BlockSpec((r, c), lambda j: (0, 0))
    lead = lambda r, c: pl.BlockSpec((1, r, c), lambda j: (j, 0, 0))
    x_conv, packed = pl.pallas_call(
        functools.partial(conv_state_kernel, width),
        grid=(blocks,),
        in_specs=[full(rows), full(8), full(KERNEL), lead(rows, hb), lead(1, hb), same(rows, n)],
        out_specs=[full(rows), full(n + 16)],
        out_shape=[
            jax.ShapeDtypeStruct((rows, cols), F32),
            jax.ShapeDtypeStruct((n + 16, cols), BF16),
        ],
        scratch_shapes=[pltpu.VMEM((rows + 8, wide), F32)],
        cost_estimate=pl.CostEstimate(
            flops=2 * rows * n * cols, bytes_accessed=8 * rows * cols, transcendentals=rows * cols
        ),
        name="conv_state",
    )(x_proj, x_before, conv_x, by_block(step * jnp.exp(total - cumul)), total3, b_mat)

    carry = passed_along(packed, "seq", 1)
    distance = 1
    while distance < lax.axis_size("seq") - 1:
        earlier = passed_along(carry, "seq", distance).astype(F32)
        mine = carry.astype(F32)
        decay = mine[n : n + 1]
        state = decay * earlier[:n] + mine[:n]
        carry = jnp.concatenate([state, decay * earlier[n:]], axis=0).astype(BF16)
        distance *= 2
    entering = carry[:n]

    y_local = pl.pallas_call(
        functools.partial(local_kernel, width),
        grid=(blocks,),
        in_specs=[
            full(rows), lead(rows, hb), lead(rows, hb), lead(hb, rows),
            same(rows, n), same(rows, n), lead(1, hb),
        ],
        out_specs=full(rows),
        out_shape=jax.ShapeDtypeStruct((rows, cols), F32),
        cost_estimate=pl.CostEstimate(
            flops=8 * rows * n * cols, bytes_accessed=8 * rows * cols, transcendentals=rows * CHUNK * heads
        ),
        name="local_ssd",
    )(
        x_conv, by_block(step), by_block(cumul), cumul.T.reshape(blocks, hb, rows),
        b_mat, c_mat, by_block(skip[None, :]),
    )
    gate_proj = dot(rows_all, w_in_z)

    gated, squares = pl.pallas_call(
        functools.partial(gate_kernel, width),
        grid=(blocks,),
        in_specs=[
            full(rows), full(rows), lead(rows, hb), same(rows, n), full(n), full(1),
        ],
        out_specs=[full(rows), same(rows, 1)],
        out_shape=[
            jax.ShapeDtypeStruct((rows, cols), BF16),
            jax.ShapeDtypeStruct((rows, 1), F32),
        ],
        cost_estimate=pl.CostEstimate(
            flops=2 * rows * n * cols, bytes_accessed=10 * rows * cols, transcendentals=rows * cols
        ),
        name="gate",
    )(y_local, gate_proj, by_block(jnp.exp(cumul)), c_mat, entering, norm_gain[None, :])
    squares = lax.psum(squares[:, 0], "head")
    scale = lax.rsqrt(squares / inner + 1e-05)
    partial = (dot(gated, w_out) * scale[:, None]).astype(BF16)
    return lax.psum_scatter(partial, "head", scatter_dimension=0, tiled=True)


def solution(mesh):
    placed = (
        P(("seq", "head"), None), P(None, "head"), P(None, "head"), P(), P(None, "head"),
        P(None, "head"), P(), P("head"), P("head"), P("head"), P("head"), P("head", None),
    )
    return jax.shard_map(
        per_device, mesh=mesh, in_specs=placed, out_specs=P(("seq", "head"), None), check_vma=False
    )
```

```python
import functools
import jax
import jax.numpy as jnp
from jax import lax
from jax.experimental import pallas as pl
from jax.experimental.pallas import tpu as pltpu
from jax.sharding import PartitionSpec as P

CHUNK = 128
KERNEL = 4
F32 = jnp.float32
BF16 = jnp.bfloat16
highest = lax.Precision.HIGHEST


def passed_along(block, axis, distance):
    devices = range(lax.axis_size(axis))
    route = [(i - distance, i) for i in devices if i - distance in devices]
    return lax.ppermute(block, axis, route)


def widen(columns, width):
    rows, heads = columns.shape
    lane = lax.broadcasted_iota(jnp.int32, (rows, 2 * width), 1)
    parts = []
    for h in range(0, heads, 2):
        left = jnp.broadcast_to(columns[:, h : h + 1], (rows, 2 * width))
        right = jnp.broadcast_to(columns[:, h + 1 : h + 2], (rows, 2 * width))
        parts.append(jnp.where(lane < width, left, right))
    return jnp.concatenate(parts, axis=1)


def conv_state_kernel(width, x_ref, before_ref, taps_ref, weight_ref, total_ref, b_ref, conv_ref, state_ref, pad_ref):
    rows = x_ref.shape[0]
    pad_ref[0:8, :] = before_ref[...]
    pad_ref[8 : 8 + rows, :] = x_ref[...]
    for r in range(0, rows, CHUNK):
        acc = taps_ref[0:1, :] * pad_ref[r + 5 : r + 5 + CHUNK, :]
        for k in range(1, KERNEL):
            acc = acc + taps_ref[k : k + 1, :] * pad_ref[r + 5 + k : r + 5 + k + CHUNK, :]
        value = acc / (1.0 + jnp.exp(-acc))
        conv_ref[r : r + CHUNK, :] = value
        fresh = (value * widen(weight_ref[0, r : r + CHUNK, :], width)).astype(BF16)
        part = lax.dot_general(
            b_ref[r : r + CHUNK, :], fresh, (((0,), (0,)), ((), ())), preferred_element_type=F32
        )
        state = part if r == 0 else state + part
    n = state.shape[0]
    state_ref[0:n, :] = state.astype(BF16)
    decay = jnp.broadcast_to(jnp.exp(total_ref[0]), (16, total_ref.shape[2]))
    state_ref[n : n + 16, :] = widen(decay, width).astype(BF16)


def local_kernel(width, x_ref, step_ref, cum_ref, cumt_ref, b_ref, c_ref, skip_ref, y_ref):
    rows, cols = x_ref.shape
    heads = cols // width
    t = lax.broadcasted_iota(jnp.int32, (CHUNK, CHUNK), 0)
    s = lax.broadcasted_iota(jnp.int32, (CHUNK, CHUNK), 1)
    lower = t >= s
    lane = lax.broadcasted_iota(jnp.int32, (CHUNK, 2 * width), 1)
    skip = widen(jnp.broadcast_to(skip_ref[0], (8, heads)), width)[0:1, :]
    state = None
    base = jnp.zeros((1, heads), F32)
    for r in range(0, rows, CHUNK):
        x = x_ref[r : r + CHUNK, :]
        b = b_ref[r : r + CHUNK, :]
        c = c_ref[r : r + CHUNK, :]
        cum = cum_ref[0, r : r + CHUNK, :]
        scaled = x * widen(step_ref[0, r : r + CHUNK, :], width)
        narrow = scaled.astype(BF16)
        scores = lax.dot_general(c, b, (((1,), (1,)), ((), ())), preferred_element_type=F32)
        scores = jnp.where(lower, scores, 0.0)
        pieces = []
        for h in range(0, heads, 2):
            pair = narrow[:, h * width : (h + 2) * width]
            both = []
            for g in (h, h + 1):
                spread = cum[:, g : g + 1] - cumt_ref[0, g : g + 1, r : r + CHUNK]
                within = scores * jnp.exp(jnp.minimum(spread, 0.0))
                both.append(jnp.dot(within.astype(BF16), pair, preferred_element_type=F32))
            pieces.append(jnp.where(lane < width, both[0], both[1]))
        y = jnp.concatenate(pieces, axis=1) + skip * x
        last = cum_ref[0, r + CHUNK - 1 : r + CHUNK, :]
        if state is not None:
            y = y + jnp.dot(c, state.astype(BF16), preferred_element_type=F32) * widen(
                jnp.exp(cum - base), width
            )
        y_ref[r : r + CHUNK, :] = y
        if r + CHUNK < rows:
            rest = (scaled * widen(jnp.exp(last - cum), width)).astype(BF16)
            fresh = lax.dot_general(b, rest, (((0,), (0,)), ((), ())), preferred_element_type=F32)
            if state is None:
                state = fresh
            else:
                kept = widen(jnp.broadcast_to(jnp.exp(last - base), (8, heads)), width)[0:1, :]
                state = kept * state + fresh
            base = last


def gate_kernel(width, y_ref, z_ref, grow_ref, c_ref, state_ref, gain_ref, out_ref, sq_ref):
    j = pl.program_id(0)

    @pl.when(j == 0)
    def _():
        sq_ref[...] = jnp.zeros_like(sq_ref)

    for r in range(0, y_ref.shape[0], CHUNK):
        at = slice(r, r + CHUNK)
        carried = jnp.dot(c_ref[at, :], state_ref[...], preferred_element_type=F32)
        ssd = y_ref[at, :] + carried * widen(grow_ref[0, at, :], width)
        z = z_ref[at, :]
        gated = ssd * (z / (1.0 + jnp.exp(-z)))
        sq_ref[at, :] += jnp.sum(gated * gated, axis=1, keepdims=True)
        out_ref[at, :] = (gated * gain_ref[...]).astype(BF16)


MESH = pl.DeviceIdType.MESH
PIECES = 4


def greet(peers):
    barrier = pltpu.get_barrier_semaphore()
    for peer in peers:
        pl.semaphore_signal(barrier, inc=1, device_id={"head": peer}, device_id_type=MESH)
    pl.semaphore_wait(barrier, len(peers))


def gather_kernel(n, x_ref, out_ref, send_own, recv_own, send_far, recv_far, send_on, recv_on):
    me = lax.axis_index("head")
    half = n // 2
    chip, core = me // 2, me % 2
    partner = chip * 2 + 1 - core
    rows = x_ref.shape[0]
    part = rows // PIECES
    far = [lax.rem(chip + d, half) * 2 + core for d in range(1, half)]
    greet([partner] + far)

    def remote(src, dst, ssem, rsem, to):
        return pltpu.make_async_remote_copy(
            src_ref=src, dst_ref=dst, send_sem=ssem, recv_sem=rsem,
            device_id={"head": to}, device_id_type=MESH,
        )

    def place(owner, q):
        return out_ref.at[pl.ds(pl.multiple_of(owner * rows + q * part, part), part), :]

    sent = []
    for q in range(PIECES):
        for d in range(1, half):
            sent.append(
                remote(x_ref.at[pl.ds(q * part, part), :], place(me, q),
                       send_far.at[d, q], recv_far.at[d, q], far[d - 1])
            )
            sent[-1].start()
    for q in range(PIECES):
        sent.append(
            remote(x_ref.at[pl.ds(q * part, part), :], place(me, q),
                   send_own.at[q], recv_own.at[q], partner)
        )
        sent[-1].start()
    out_ref[pl.ds(pl.multiple_of(me * rows, rows), rows), :] = x_ref[...]
    passed = []
    for q in range(PIECES):
        for d in range(1, half):
            owner = lax.rem(chip - d + half, half) * 2 + core
            remote(place(owner, q), place(owner, q), send_far.at[d, q], recv_far.at[d, q], partner).wait_recv()
            passed.append(
                remote(place(owner, q), place(owner, q), send_on.at[d, q], recv_on.at[d, q], partner)
            )
            passed[-1].start()
    for copy in sent:
        copy.wait_send()
    for q in range(PIECES):
        remote(place(partner, q), place(partner, q), send_own.at[q], recv_own.at[q], partner).wait_recv()
    for copy in passed:
        copy.wait_send()
    for q in range(PIECES):
        for d in range(1, half):
            owner = lax.rem(chip - d + half, half) * 2 + 1 - core
            remote(place(owner, q), place(owner, q), send_on.at[d, q], recv_on.at[d, q], partner).wait_recv()


def gather_tokens(tokens, n):
    rows, depth = tokens.shape
    half = n // 2
    dma = pltpu.SemaphoreType.DMA
    return pl.pallas_call(
        functools.partial(gather_kernel, n),
        out_shape=jax.ShapeDtypeStruct((rows * n, depth), tokens.dtype),
        in_specs=[pl.BlockSpec(memory_space=pltpu.VMEM)],
        out_specs=pl.BlockSpec(memory_space=pltpu.VMEM),
        scratch_shapes=[dma((PIECES,)), dma((PIECES,))] + [dma((half, PIECES))] * 4,
        compiler_params=pltpu.CompilerParams(collective_id=0, has_side_effects=True),
        name="gather_tokens",
    )(tokens)


def scatter_kernel(n, p_ref, sq_ref, out_ref, total_ref, got, summed, landed, squares, s1, r1, s2, r2, s3, r3):
    me = lax.axis_index("head")
    half = n // 2
    chip, core = me // 2, me % 2
    partner = chip * 2 + 1 - core
    rows = out_ref.shape[0]
    part = rows // PIECES
    peers = [lax.rem(me + d, n) for d in range(1, n)]
    greet(peers)

    def remote(src, dst, ssem, rsem, to):
        return pltpu.make_async_remote_copy(
            src_ref=src, dst_ref=dst, send_sem=ssem, recv_sem=rsem,
            device_id={"head": to}, device_id_type=MESH,
        )

    def block(owner, q):
        return p_ref.at[pl.ds(pl.multiple_of(owner * rows + q * part, part), part), :]

    def piece(ref, d, q):
        return ref.at[d, pl.ds(q * part, part), :]

    sent = []
    for d in list(range(1, half)) + [0]:
        for q in range(PIECES):
            owner = lax.rem(chip + d, half) * 2 + 1 - core
            sent.append(remote(block(owner, q), piece(got, d, q), s1.at[d, q], r1.at[d, q], partner))
            sent[-1].start()
    for d in range(1, n):
        sent.append(remote(sq_ref.at[peers[d - 1]], squares.at[d], s3.at[d], r3.at[d], peers[d - 1]))
        sent[-1].start()
    for d in range(1, half):
        for q in range(PIECES):
            owner = lax.rem(chip + d, half) * 2 + core
            remote(piece(got, d, q), piece(got, d, q), s1.at[d, q], r1.at[d, q], partner).wait_recv()
            both = block(owner, q)[...].astype(F32) + piece(got, d, q)[...].astype(F32)
            summed[d, q * part : (q + 1) * part, :] = both.astype(BF16)
            sent.append(remote(piece(summed, d, q), piece(landed, d, q), s2.at[d, q], r2.at[d, q], owner))
            sent[-1].start()
    total = sq_ref[me]
    for d in range(1, n):
        remote(squares.at[d], squares.at[d], s3.at[d], r3.at[d], partner).wait_recv()
        total = total + squares[d]
    total_ref[...] = total
    for q in range(PIECES):
        remote(piece(got, 0, q), piece(got, 0, q), s1.at[0, q], r1.at[0, q], partner).wait_recv()
        out_ref[q * part : (q + 1) * part, :] = (
            block(me, q)[...].astype(F32) + piece(got, 0, q)[...].astype(F32)
        )
    for q in range(PIECES):
        for d in range(1, half):
            remote(piece(landed, d, q), piece(landed, d, q), s2.at[d, q], r2.at[d, q], partner).wait_recv()
            out_ref[q * part : (q + 1) * part, :] += piece(landed, d, q)[...].astype(F32)
    for copy in sent:
        copy.wait_send()


def scatter_sum(partial, squares, n):
    rows, depth = partial.shape
    rows = rows // n
    half = n // 2
    dma = pltpu.SemaphoreType.DMA
    vmem = pl.BlockSpec(memory_space=pltpu.VMEM)
    squares = jnp.broadcast_to(squares.reshape(n, 1, rows), (n, 8, rows))
    return pl.pallas_call(
        functools.partial(scatter_kernel, n),
        out_shape=[
            jax.ShapeDtypeStruct((rows, depth), F32),
            jax.ShapeDtypeStruct((8, rows), F32),
        ],
        in_specs=[vmem, vmem],
        out_specs=[vmem, vmem],
        scratch_shapes=[pltpu.VMEM((half, rows, depth), BF16)] * 3
        + [pltpu.VMEM((n, 8, rows), F32)]
        + [dma((half, PIECES))] * 4
        + [dma((n,))] * 2,
        compiler_params=pltpu.CompilerParams(collective_id=1, has_side_effects=True),
        name="scatter_sum",
    )(partial, squares)


def per_device(
    tokens, w_in_x, w_in_z, w_in_bc, w_dt, conv_x, conv_bc, dt_bias, decay_rate, skip, norm_gain, w_out
):
    cols = w_in_x.shape[1]
    heads = dt_bias.shape[0]
    width = cols // heads
    n = w_in_bc.shape[1] // 2
    inner = cols * lax.axis_size("head")
    rows_all = gather_tokens(tokens, lax.axis_size("head"))
    rows = rows_all.shape[0]
    dot = functools.partial(jnp.dot, preferred_element_type=F32)
    x_proj = dot(rows_all, w_in_x)
    small = dot(rows_all, jnp.concatenate([w_in_bc, w_dt], axis=1))
    bc_proj, step_raw = small[:, : 2 * n], small[:, 2 * n :]
    before = passed_along(
        jnp.concatenate([x_proj[-8:], bc_proj[-8:]], axis=1), "seq", 1
    )
    x_before, bc_before = before[:, :cols], before[:, cols:]
    padded = jnp.concatenate([bc_before, bc_proj], axis=0)
    bc = sum(conv_bc[k] * padded[5 + k : 5 + k + rows] for k in range(KERNEL))
    bc = jax.nn.silu(bc).astype(BF16)
    b_mat, c_mat = bc[:, :n], bc[:, n:]
    step = jax.nn.softplus(step_raw + dt_bias)
    order = jnp.arange(rows)
    tri = (order[:, None] >= order[None, :]).astype(F32)
    cumul = jnp.dot(tri, -step * decay_rate, precision=highest)
    total = cumul[-1:]

    hb = min(heads, 256 // width)
    blocks = heads // hb
    wide = hb * width

    def by_block(a):
        return a.reshape(a.shape[0], blocks, hb).transpose(1, 0, 2)

    total3 = by_block(total)
    full = lambda r: pl.BlockSpec((r, wide), lambda j: (0, j))
    same = lambda r, c: pl.BlockSpec((r, c), lambda j: (0, 0))
    lead = lambda r, c: pl.BlockSpec((1, r, c), lambda j: (j, 0, 0))
    x_conv, packed = pl.pallas_call(
        functools.partial(conv_state_kernel, width),
        grid=(blocks,),
        in_specs=[full(rows), full(8), full(KERNEL), lead(rows, hb), lead(1, hb), same(rows, n)],
        out_specs=[full(rows), full(n + 16)],
        out_shape=[
            jax.ShapeDtypeStruct((rows, cols), F32),
            jax.ShapeDtypeStruct((n + 16, cols), BF16),
        ],
        scratch_shapes=[pltpu.VMEM((rows + 8, wide), F32)],
        cost_estimate=pl.CostEstimate(
            flops=2 * rows * n * cols, bytes_accessed=8 * rows * cols, transcendentals=rows * cols
        ),
        name="conv_state",
    )(x_proj, x_before, conv_x, by_block(step * jnp.exp(total - cumul)), total3, b_mat)

    y_local = pl.pallas_call(
        functools.partial(local_kernel, width),
        grid=(blocks,),
        in_specs=[
            full(rows), lead(rows, hb), lead(rows, hb), lead(hb, rows),
            same(rows, n), same(rows, n), lead(1, hb),
        ],
        out_specs=full(rows),
        out_shape=jax.ShapeDtypeStruct((rows, cols), F32),
        cost_estimate=pl.CostEstimate(
            flops=8 * rows * n * cols, bytes_accessed=8 * rows * cols, transcendentals=rows * CHUNK * heads
        ),
        name="local_ssd",
    )(
        x_conv, by_block(step), by_block(cumul), cumul.T.reshape(blocks, hb, rows),
        b_mat, c_mat, by_block(skip[None, :]),
    )
    gate_proj = dot(rows_all, w_in_z)
    fillers = [y_local, gate_proj]
    carry = passed_along(packed, "seq", 1)
    distance = 1
    while distance < lax.axis_size("seq") - 1:
        if fillers:
            carry, done = lax.optimization_barrier((carry, fillers.pop(0)))
            y_local, gate_proj = (done, gate_proj) if distance == 1 else (y_local, done)
        earlier = passed_along(carry, "seq", distance).astype(F32)
        mine = carry.astype(F32)
        decay = mine[n : n + 1]
        state = decay * earlier[:n] + mine[:n]
        carry = jnp.concatenate([state, decay * earlier[n:]], axis=0).astype(BF16)
        distance *= 2
    entering = carry[:n]

    gated, squares = pl.pallas_call(
        functools.partial(gate_kernel, width),
        grid=(blocks,),
        in_specs=[
            full(rows), full(rows), lead(rows, hb), same(rows, n), full(n), full(1),
        ],
        out_specs=[full(rows), same(rows, 1)],
        out_shape=[
            jax.ShapeDtypeStruct((rows, cols), BF16),
            jax.ShapeDtypeStruct((rows, 1), F32),
        ],
        cost_estimate=pl.CostEstimate(
            flops=2 * rows * n * cols, bytes_accessed=10 * rows * cols, transcendentals=rows * cols
        ),
        name="gate",
    )(y_local, gate_proj, by_block(jnp.exp(cumul)), c_mat, entering, norm_gain[None, :])
    mixed, squares = scatter_sum(dot(gated, w_out).astype(BF16), squares[:, 0], lax.axis_size("head"))
    scale = lax.rsqrt(squares[0] / inner + 1e-05)
    return (mixed * scale[:, None]).astype(BF16)


def solution(mesh):
    placed = (
        P(("seq", "head"), None), P(None, "head"), P(None, "head"), P(), P(None, "head"),
        P(None, "head"), P(), P("head"), P("head"), P("head"), P("head"), P("head", None),
    )
    return jax.shard_map(
        per_device, mesh=mesh, in_specs=placed, out_specs=P(("seq", "head"), None), check_vma=False
    )
```

```python
import functools
import jax
import jax.numpy as jnp
from jax import lax
from jax.experimental import pallas as pl
from jax.experimental.pallas import tpu as pltpu
from jax.sharding import PartitionSpec as P

CHUNK = 128
KERNEL = 4
F32 = jnp.float32
BF16 = jnp.bfloat16
highest = lax.Precision.HIGHEST


def passed_along(block, axis, distance):
    devices = range(lax.axis_size(axis))
    route = [(i - distance, i) for i in devices if i - distance in devices]
    return lax.ppermute(block, axis, route)


def widen(columns, width):
    rows, heads = columns.shape
    lane = lax.broadcasted_iota(jnp.int32, (rows, 2 * width), 1)
    parts = []
    for h in range(0, heads, 2):
        left = jnp.broadcast_to(columns[:, h : h + 1], (rows, 2 * width))
        right = jnp.broadcast_to(columns[:, h + 1 : h + 2], (rows, 2 * width))
        parts.append(jnp.where(lane < width, left, right))
    return jnp.concatenate(parts, axis=1)


def conv_state_kernel(width, x_ref, before_ref, taps_ref, weight_ref, total_ref, b_ref, conv_ref, state_ref, pad_ref):
    rows = x_ref.shape[0]
    pad_ref[0:8, :] = before_ref[...]
    pad_ref[8 : 8 + rows, :] = x_ref[...]
    for r in range(0, rows, CHUNK):
        acc = taps_ref[0:1, :] * pad_ref[r + 5 : r + 5 + CHUNK, :]
        for k in range(1, KERNEL):
            acc = acc + taps_ref[k : k + 1, :] * pad_ref[r + 5 + k : r + 5 + k + CHUNK, :]
        value = acc / (1.0 + jnp.exp(-acc))
        conv_ref[r : r + CHUNK, :] = value
        fresh = (value * widen(weight_ref[0, r : r + CHUNK, :], width)).astype(BF16)
        part = lax.dot_general(
            b_ref[r : r + CHUNK, :], fresh, (((0,), (0,)), ((), ())), preferred_element_type=F32
        )
        state = part if r == 0 else state + part
    n = state.shape[0]
    state_ref[0:n, :] = state.astype(BF16)
    decay = jnp.broadcast_to(jnp.exp(total_ref[0]), (16, total_ref.shape[2]))
    state_ref[n : n + 16, :] = widen(decay, width).astype(BF16)


def local_kernel(width, x_ref, step_ref, cum_ref, cumt_ref, b_ref, c_ref, skip_ref, y_ref):
    rows, cols = x_ref.shape
    heads = cols // width
    t = lax.broadcasted_iota(jnp.int32, (CHUNK, CHUNK), 0)
    s = lax.broadcasted_iota(jnp.int32, (CHUNK, CHUNK), 1)
    lower = t >= s
    lane = lax.broadcasted_iota(jnp.int32, (CHUNK, 2 * width), 1)
    skip = widen(jnp.broadcast_to(skip_ref[0], (8, heads)), width)[0:1, :]
    state = None
    base = jnp.zeros((1, heads), F32)
    for r in range(0, rows, CHUNK):
        x = x_ref[r : r + CHUNK, :]
        b = b_ref[r : r + CHUNK, :]
        c = c_ref[r : r + CHUNK, :]
        cum = cum_ref[0, r : r + CHUNK, :]
        scaled = x * widen(step_ref[0, r : r + CHUNK, :], width)
        narrow = scaled.astype(BF16)
        scores = lax.dot_general(c, b, (((1,), (1,)), ((), ())), preferred_element_type=F32)
        scores = jnp.where(lower, scores, 0.0)
        pieces = []
        for h in range(0, heads, 2):
            pair = narrow[:, h * width : (h + 2) * width]
            both = []
            for g in (h, h + 1):
                spread = cum[:, g : g + 1] - cumt_ref[0, g : g + 1, r : r + CHUNK]
                within = scores * jnp.exp(jnp.minimum(spread, 0.0))
                both.append(jnp.dot(within.astype(BF16), pair, preferred_element_type=F32))
            pieces.append(jnp.where(lane < width, both[0], both[1]))
        y = jnp.concatenate(pieces, axis=1) + skip * x
        last = cum_ref[0, r + CHUNK - 1 : r + CHUNK, :]
        if state is not None:
            y = y + jnp.dot(c, state.astype(BF16), preferred_element_type=F32) * widen(
                jnp.exp(cum - base), width
            )
        y_ref[r : r + CHUNK, :] = y
        if r + CHUNK < rows:
            rest = (scaled * widen(jnp.exp(last - cum), width)).astype(BF16)
            fresh = lax.dot_general(b, rest, (((0,), (0,)), ((), ())), preferred_element_type=F32)
            if state is None:
                state = fresh
            else:
                kept = widen(jnp.broadcast_to(jnp.exp(last - base), (8, heads)), width)[0:1, :]
                state = kept * state + fresh
            base = last


def gate_block(width, y_ref, z_ref, cum_ref, c_ref, state_ref, gain_ref, out_ref, sq_ref):
    for r in range(0, y_ref.shape[0], CHUNK):
        at = slice(r, r + CHUNK)
        carried = jnp.dot(c_ref[at, :], state_ref[...], preferred_element_type=F32)
        ssd = y_ref[at, :] + carried * widen(jnp.exp(cum_ref[0, at, :]), width)
        z = z_ref[at, :]
        gated = ssd * (z / (1.0 + jnp.exp(-z)))
        sq_ref[at, :] += jnp.sum(gated * gated, axis=1, keepdims=True)
        out_ref[at, :] = (gated * gain_ref[...]).astype(BF16)


MESH = pl.DeviceIdType.MESH
PIECES = 4


def greet(peers):
    barrier = pltpu.get_barrier_semaphore()
    for peer in peers:
        pl.semaphore_signal(barrier, inc=1, device_id={"head": peer}, device_id_type=MESH)
    pl.semaphore_wait(barrier, len(peers))


def gather_kernel(n, x_ref, out_ref, send_own, recv_own, send_far, recv_far, send_on, recv_on):
    me = lax.axis_index("head")
    half = n // 2
    chip, core = me // 2, me % 2
    partner = chip * 2 + 1 - core
    rows = x_ref.shape[0]
    part = rows // PIECES
    far = [lax.rem(chip + d, half) * 2 + core for d in range(1, half)]
    greet([partner] + far)

    def remote(src, dst, ssem, rsem, to):
        return pltpu.make_async_remote_copy(
            src_ref=src, dst_ref=dst, send_sem=ssem, recv_sem=rsem,
            device_id={"head": to}, device_id_type=MESH,
        )

    def place(owner, q):
        return out_ref.at[pl.ds(pl.multiple_of(owner * rows + q * part, part), part), :]

    sent = []
    for q in range(PIECES):
        for d in range(1, half):
            sent.append(
                remote(x_ref.at[pl.ds(q * part, part), :], place(me, q),
                       send_far.at[d, q], recv_far.at[d, q], far[d - 1])
            )
            sent[-1].start()
    for q in range(PIECES):
        sent.append(
            remote(x_ref.at[pl.ds(q * part, part), :], place(me, q),
                   send_own.at[q], recv_own.at[q], partner)
        )
        sent[-1].start()
    out_ref[pl.ds(pl.multiple_of(me * rows, rows), rows), :] = x_ref[...]
    passed = []
    for q in range(PIECES):
        for d in range(1, half):
            owner = lax.rem(chip - d + half, half) * 2 + core
            remote(place(owner, q), place(owner, q), send_far.at[d, q], recv_far.at[d, q], partner).wait_recv()
            passed.append(
                remote(place(owner, q), place(owner, q), send_on.at[d, q], recv_on.at[d, q], partner)
            )
            passed[-1].start()
    for copy in sent:
        copy.wait_send()
    for q in range(PIECES):
        remote(place(partner, q), place(partner, q), send_own.at[q], recv_own.at[q], partner).wait_recv()
    for copy in passed:
        copy.wait_send()
    for q in range(PIECES):
        for d in range(1, half):
            owner = lax.rem(chip - d + half, half) * 2 + 1 - core
            remote(place(owner, q), place(owner, q), send_on.at[d, q], recv_on.at[d, q], partner).wait_recv()


def gather_tokens(tokens, n):
    rows, depth = tokens.shape
    half = n // 2
    dma = pltpu.SemaphoreType.DMA
    return pl.pallas_call(
        functools.partial(gather_kernel, n),
        out_shape=jax.ShapeDtypeStruct((rows * n, depth), tokens.dtype),
        in_specs=[pl.BlockSpec(memory_space=pltpu.VMEM)],
        out_specs=pl.BlockSpec(memory_space=pltpu.VMEM),
        scratch_shapes=[dma((PIECES,)), dma((PIECES,))] + [dma((half, PIECES))] * 4,
        compiler_params=pltpu.CompilerParams(collective_id=0, has_side_effects=True),
        name="gather_tokens",
    )(tokens)


def scatter_kernel(n, p_ref, sq_ref, out_ref, total_ref, got, summed, landed, squares, s1, r1, s2, r2, s3, r3):
    me = lax.axis_index("head")
    half = n // 2
    chip, core = me // 2, me % 2
    partner = chip * 2 + 1 - core
    rows = out_ref.shape[0]
    part = rows // PIECES
    peers = [lax.rem(me + d, n) for d in range(1, n)]
    greet(peers)

    def remote(src, dst, ssem, rsem, to):
        return pltpu.make_async_remote_copy(
            src_ref=src, dst_ref=dst, send_sem=ssem, recv_sem=rsem,
            device_id={"head": to}, device_id_type=MESH,
        )

    def block(owner, q):
        return p_ref.at[pl.ds(pl.multiple_of(owner * rows + q * part, part), part), :]

    def piece(ref, d, q):
        return ref.at[d, pl.ds(q * part, part), :]

    sent = []
    for d in list(range(1, half)) + [0]:
        for q in range(PIECES):
            owner = lax.rem(chip + d, half) * 2 + 1 - core
            sent.append(remote(block(owner, q), piece(got, d, q), s1.at[d, q], r1.at[d, q], partner))
            sent[-1].start()
    for d in range(1, n):
        sent.append(remote(sq_ref.at[peers[d - 1]], squares.at[d], s3.at[d], r3.at[d], peers[d - 1]))
        sent[-1].start()
    for d in range(1, half):
        for q in range(PIECES):
            owner = lax.rem(chip + d, half) * 2 + core
            remote(piece(got, d, q), piece(got, d, q), s1.at[d, q], r1.at[d, q], partner).wait_recv()
            both = block(owner, q)[...].astype(F32) + piece(got, d, q)[...].astype(F32)
            summed[d, q * part : (q + 1) * part, :] = both.astype(BF16)
            sent.append(remote(piece(summed, d, q), piece(landed, d, q), s2.at[d, q], r2.at[d, q], owner))
            sent[-1].start()
    total = sq_ref[me]
    for d in range(1, n):
        remote(squares.at[d], squares.at[d], s3.at[d], r3.at[d], partner).wait_recv()
        total = total + squares[d]
    total_ref[...] = total
    for q in range(PIECES):
        remote(piece(got, 0, q), piece(got, 0, q), s1.at[0, q], r1.at[0, q], partner).wait_recv()
        out_ref[q * part : (q + 1) * part, :] = (
            block(me, q)[...].astype(F32) + piece(got, 0, q)[...].astype(F32)
        )
    for q in range(PIECES):
        for d in range(1, half):
            remote(piece(landed, d, q), piece(landed, d, q), s2.at[d, q], r2.at[d, q], partner).wait_recv()
            out_ref[q * part : (q + 1) * part, :] += piece(landed, d, q)[...].astype(F32)
    for copy in sent:
        copy.wait_send()


def scatter_sum(partial, squares, n):
    rows, depth = partial.shape
    rows = rows // n
    half = n // 2
    dma = pltpu.SemaphoreType.DMA
    vmem = pl.BlockSpec(memory_space=pltpu.VMEM)
    squares = jnp.broadcast_to(squares.reshape(n, 1, rows), (n, 8, rows))
    return pl.pallas_call(
        functools.partial(scatter_kernel, n),
        out_shape=[
            jax.ShapeDtypeStruct((rows, depth), F32),
            jax.ShapeDtypeStruct((8, rows), F32),
        ],
        in_specs=[vmem, vmem],
        out_specs=[vmem, vmem],
        scratch_shapes=[pltpu.VMEM((half, rows, depth), BF16)] * 3
        + [pltpu.VMEM((n, 8, rows), F32)]
        + [dma((half, PIECES))] * 4
        + [dma((n,))] * 2,
        compiler_params=pltpu.CompilerParams(collective_id=1, has_side_effects=True),
        name="scatter_sum",
    )(partial, squares)


def chain_kernel(
    n_seq, width, packed_ref, rows_ref, wz_ref, x_ref, step_ref, cum_ref, cumt_ref, b_ref, c_ref,
    skip_ref, gain_ref, out_ref, sq_ref, y_ref, z_ref, held, came, send_sem, recv_sem,
):
    me = lax.axis_index("seq")
    n = b_ref.shape[1]
    blocks, _, hb = step_ref.shape
    wide = hb * width
    steps = [1]
    while 2 * steps[-1] < n_seq:
        steps.append(2 * steps[-1])
    barrier = pltpu.get_barrier_semaphore()
    for d in steps:
        for peer in (lax.rem(me + d, n_seq), lax.rem(me - d + n_seq, n_seq)):
            pl.semaphore_signal(barrier, inc=1, device_id={"seq": peer}, device_id_type=MESH)
    pl.semaphore_wait(barrier, 2 * len(steps))

    def z_unit(j):
        z_ref[:, j * wide : (j + 1) * wide] = jnp.dot(
            rows_ref[...], wz_ref[:, j * wide : (j + 1) * wide], preferred_element_type=F32
        )

    def local_unit(j):
        at = pl.ds(j * wide, wide)
        one = pl.ds(j, 1)
        local_kernel(
            width, x_ref.at[:, at], step_ref.at[one], cum_ref.at[one], cumt_ref.at[one],
            b_ref, c_ref, skip_ref.at[one], y_ref.at[:, at],
        )

    units = [functools.partial(f, j) for j in range(blocks) for f in (local_unit, z_unit)]
    distances = [1] + steps
    for k, d in enumerate(distances):
        copy = pltpu.make_async_remote_copy(
            src_ref=packed_ref if k == 0 else held.at[k],
            dst_ref=came.at[k], send_sem=send_sem.at[k], recv_sem=recv_sem.at[k],
            device_id={"seq": lax.rem(me + d, n_seq)}, device_id_type=MESH,
        )
        copy.start()
        first = k * len(units) // len(distances)
        for unit in units[first : (k + 1) * len(units) // len(distances)]:
            unit()
        copy.wait()
        valid = (me >= d).astype(F32)
        for j in range(blocks):
            at = slice(j * wide, (j + 1) * wide)
            earlier = came[k, :, at].astype(F32) * valid
            if k > 0:
                mine = held[k, :, at].astype(F32)
                decay = mine[n : n + 1]
                earlier = jnp.concatenate([decay * earlier[:n] + mine[:n], decay * earlier[n:]], axis=0)
            held[k + 1, :, at] = earlier.astype(BF16)
    sq_ref[...] = jnp.zeros_like(sq_ref)
    entering = held.at[len(distances)]
    for j in range(blocks):
        at = pl.ds(j * wide, wide)
        gate_block(
            width, y_ref.at[:, at], z_ref.at[:, at], cum_ref.at[pl.ds(j, 1)], c_ref,
            entering.at[pl.ds(0, n), at], gain_ref.at[:, at], out_ref.at[:, at], sq_ref,
        )


def per_device(
    tokens, w_in_x, w_in_z, w_in_bc, w_dt, conv_x, conv_bc, dt_bias, decay_rate, skip, norm_gain, w_out
):
    cols = w_in_x.shape[1]
    heads = dt_bias.shape[0]
    width = cols // heads
    n = w_in_bc.shape[1] // 2
    inner = cols * lax.axis_size("head")
    rows_all = gather_tokens(tokens, lax.axis_size("head"))
    rows = rows_all.shape[0]
    dot = functools.partial(jnp.dot, preferred_element_type=F32)
    x_proj = dot(rows_all, w_in_x)
    small = dot(rows_all, jnp.concatenate([w_in_bc, w_dt], axis=1))
    bc_proj, step_raw = small[:, : 2 * n], small[:, 2 * n :]
    before = passed_along(
        jnp.concatenate([x_proj[-8:], bc_proj[-8:]], axis=1), "seq", 1
    )
    x_before, bc_before = before[:, :cols], before[:, cols:]
    padded = jnp.concatenate([bc_before, bc_proj], axis=0)
    bc = sum(conv_bc[k] * padded[5 + k : 5 + k + rows] for k in range(KERNEL))
    bc = jax.nn.silu(bc).astype(BF16)
    b_mat, c_mat = bc[:, :n], bc[:, n:]
    step = jax.nn.softplus(step_raw + dt_bias)
    order = jnp.arange(rows)
    tri = (order[:, None] >= order[None, :]).astype(F32)
    cumul = jnp.dot(tri, -step * decay_rate, precision=highest)
    total = cumul[-1:]

    hb = min(heads, 256 // width)
    blocks = heads // hb
    wide = hb * width

    def by_block(a):
        return a.reshape(a.shape[0], blocks, hb).transpose(1, 0, 2)

    total3 = by_block(total)
    full = lambda r: pl.BlockSpec((r, wide), lambda j: (0, j))
    same = lambda r, c: pl.BlockSpec((r, c), lambda j: (0, 0))
    lead = lambda r, c: pl.BlockSpec((1, r, c), lambda j: (j, 0, 0))
    x_conv, packed = pl.pallas_call(
        functools.partial(conv_state_kernel, width),
        grid=(blocks,),
        in_specs=[full(rows), full(8), full(KERNEL), lead(rows, hb), lead(1, hb), same(rows, n)],
        out_specs=[full(rows), full(n + 16)],
        out_shape=[
            jax.ShapeDtypeStruct((rows, cols), F32),
            jax.ShapeDtypeStruct((n + 16, cols), BF16),
        ],
        scratch_shapes=[pltpu.VMEM((rows + 8, wide), F32)],
        cost_estimate=pl.CostEstimate(
            flops=2 * rows * n * cols, bytes_accessed=8 * rows * cols, transcendentals=rows * cols
        ),
        name="conv_state",
    )(x_proj, x_before, conv_x, by_block(step * jnp.exp(total - cumul)), total3, b_mat)

    n_seq = lax.axis_size("seq")
    stages = 1 + max(1, (n_seq - 1).bit_length())
    vmem = pl.BlockSpec(memory_space=pltpu.VMEM)
    gated, squares = pl.pallas_call(
        functools.partial(chain_kernel, n_seq, width),
        out_shape=[
            jax.ShapeDtypeStruct((rows, cols), BF16),
            jax.ShapeDtypeStruct((rows, 1), F32),
        ],
        in_specs=[vmem] * 11,
        out_specs=[vmem, vmem],
        scratch_shapes=[
            pltpu.VMEM((rows, cols), F32),
            pltpu.VMEM((rows, cols), F32),
            pltpu.VMEM((stages + 1, n + 16, cols), BF16),
            pltpu.VMEM((stages, n + 16, cols), BF16),
            pltpu.SemaphoreType.DMA((stages,)),
            pltpu.SemaphoreType.DMA((stages,)),
        ],
        compiler_params=pltpu.CompilerParams(collective_id=2, has_side_effects=True),
        name="state_chain",
    )(
        packed, rows_all, w_in_z, x_conv, by_block(step), by_block(cumul),
        cumul.T.reshape(blocks, hb, rows), b_mat, c_mat, by_block(skip[None, :]), norm_gain[None, :],
    )
    mixed, squares = scatter_sum(dot(gated, w_out).astype(BF16), squares[:, 0], lax.axis_size("head"))
    scale = lax.rsqrt(squares[0] / inner + 1e-05)
    return (mixed * scale[:, None]).astype(BF16)


def solution(mesh):
    placed = (
        P(("seq", "head"), None), P(None, "head"), P(None, "head"), P(), P(None, "head"),
        P(None, "head"), P(), P("head"), P("head"), P("head"), P("head"), P("head", None),
    )
    return jax.shard_map(
        per_device, mesh=mesh, in_specs=placed, out_specs=P(("seq", "head"), None), check_vma=False
    )
```

```python
import functools
import jax
import jax.numpy as jnp
from jax import lax
from jax.experimental import pallas as pl
from jax.experimental.pallas import tpu as pltpu
from jax.sharding import PartitionSpec as P

CHUNK = 128
KERNEL = 4
F32 = jnp.float32
BF16 = jnp.bfloat16
highest = lax.Precision.HIGHEST


def passed_along(block, axis, distance):
    devices = range(lax.axis_size(axis))
    route = [(i - distance, i) for i in devices if i - distance in devices]
    return lax.ppermute(block, axis, route)


def widen(columns, width):
    rows, heads = columns.shape
    lane = lax.broadcasted_iota(jnp.int32, (rows, 2 * width), 1)
    parts = []
    for h in range(0, heads, 2):
        left = jnp.broadcast_to(columns[:, h : h + 1], (rows, 2 * width))
        right = jnp.broadcast_to(columns[:, h + 1 : h + 2], (rows, 2 * width))
        parts.append(jnp.where(lane < width, left, right))
    return jnp.concatenate(parts, axis=1)


def conv_state_kernel(width, x_ref, before_ref, taps_ref, weight_ref, total_ref, b_ref, conv_ref, state_ref, pad_ref):
    rows = x_ref.shape[0]
    pad_ref[0:8, :] = before_ref[...]
    pad_ref[8 : 8 + rows, :] = x_ref[...]
    for r in range(0, rows, CHUNK):
        acc = taps_ref[0:1, :] * pad_ref[r + 5 : r + 5 + CHUNK, :]
        for k in range(1, KERNEL):
            acc = acc + taps_ref[k : k + 1, :] * pad_ref[r + 5 + k : r + 5 + k + CHUNK, :]
        value = acc / (1.0 + jnp.exp(-acc))
        conv_ref[r : r + CHUNK, :] = value
        fresh = (value * widen(weight_ref[0, r : r + CHUNK, :], width)).astype(BF16)
        part = lax.dot_general(
            b_ref[r : r + CHUNK, :], fresh, (((0,), (0,)), ((), ())), preferred_element_type=F32
        )
        state = part if r == 0 else state + part
    n = state.shape[0]
    state_ref[0:n, :] = state.astype(BF16)
    decay = jnp.broadcast_to(jnp.exp(total_ref[0]), (16, total_ref.shape[2]))
    state_ref[n : n + 16, :] = widen(decay, width).astype(BF16)


def local_kernel(width, x_ref, step_ref, cum_ref, cumt_ref, b_ref, c_ref, skip_ref, y_ref):
    rows, cols = x_ref.shape
    heads = cols // width
    t = lax.broadcasted_iota(jnp.int32, (CHUNK, CHUNK), 0)
    s = lax.broadcasted_iota(jnp.int32, (CHUNK, CHUNK), 1)
    lower = t >= s
    lane = lax.broadcasted_iota(jnp.int32, (CHUNK, 2 * width), 1)
    skip = widen(jnp.broadcast_to(skip_ref[0], (8, heads)), width)[0:1, :]
    state = None
    base = jnp.zeros((1, heads), F32)
    for r in range(0, rows, CHUNK):
        x = x_ref[r : r + CHUNK, :]
        b = b_ref[r : r + CHUNK, :]
        c = c_ref[r : r + CHUNK, :]
        cum = cum_ref[0, r : r + CHUNK, :]
        scaled = x * widen(step_ref[0, r : r + CHUNK, :], width)
        narrow = scaled.astype(BF16)
        scores = lax.dot_general(c, b, (((1,), (1,)), ((), ())), preferred_element_type=F32)
        scores = jnp.where(lower, scores, 0.0)
        pieces = []
        for h in range(0, heads, 2):
            pair = narrow[:, h * width : (h + 2) * width]
            both = []
            for g in (h, h + 1):
                spread = cum[:, g : g + 1] - cumt_ref[0, g : g + 1, r : r + CHUNK]
                within = scores * jnp.exp(jnp.minimum(spread, 0.0))
                both.append(jnp.dot(within.astype(BF16), pair, preferred_element_type=F32))
            pieces.append(jnp.where(lane < width, both[0], both[1]))
        y = jnp.concatenate(pieces, axis=1) + skip * x
        last = cum_ref[0, r + CHUNK - 1 : r + CHUNK, :]
        if state is not None:
            y = y + jnp.dot(c, state.astype(BF16), preferred_element_type=F32) * widen(
                jnp.exp(cum - base), width
            )
        y_ref[r : r + CHUNK, :] = y
        if r + CHUNK < rows:
            rest = (scaled * widen(jnp.exp(last - cum), width)).astype(BF16)
            fresh = lax.dot_general(b, rest, (((0,), (0,)), ((), ())), preferred_element_type=F32)
            if state is None:
                state = fresh
            else:
                kept = widen(jnp.broadcast_to(jnp.exp(last - base), (8, heads)), width)[0:1, :]
                state = kept * state + fresh
            base = last


def gate_block(width, y_ref, z_ref, cum_ref, c_ref, state_ref, gain_ref, out_ref, sq_ref):
    for r in range(0, y_ref.shape[0], CHUNK):
        at = slice(r, r + CHUNK)
        carried = jnp.dot(c_ref[at, :], state_ref[...], preferred_element_type=F32)
        ssd = y_ref[at, :] + carried * widen(jnp.exp(cum_ref[0, at, :]), width)
        z = z_ref[at, :]
        gated = ssd * (z / (1.0 + jnp.exp(-z)))
        sq_ref[at, :] += jnp.sum(gated * gated, axis=1, keepdims=True)
        out_ref[at, :] = (gated * gain_ref[...]).astype(BF16)


MESH = pl.DeviceIdType.MESH
PIECES = 4


def greet(peers):
    barrier = pltpu.get_barrier_semaphore()
    for peer in peers:
        pl.semaphore_signal(barrier, inc=1, device_id={"head": peer}, device_id_type=MESH)
    pl.semaphore_wait(barrier, len(peers))


def gather_kernel(n, x_ref, out_ref, send_own, recv_own, send_far, recv_far, send_on, recv_on):
    me = lax.axis_index("head")
    half = n // 2
    chip, core = me // 2, me % 2
    partner = chip * 2 + 1 - core
    rows = x_ref.shape[0]
    part = rows // PIECES
    far = [lax.rem(chip + d, half) * 2 + core for d in range(1, half)]
    greet([partner] + far)

    def remote(src, dst, ssem, rsem, to):
        return pltpu.make_async_remote_copy(
            src_ref=src, dst_ref=dst, send_sem=ssem, recv_sem=rsem,
            device_id={"head": to}, device_id_type=MESH,
        )

    def place(owner, q):
        return out_ref.at[pl.ds(pl.multiple_of(owner * rows + q * part, part), part), :]

    sent = []
    for q in range(PIECES):
        for d in range(1, half):
            sent.append(
                remote(x_ref.at[pl.ds(q * part, part), :], place(me, q),
                       send_far.at[d, q], recv_far.at[d, q], far[d - 1])
            )
            sent[-1].start()
    for q in range(PIECES):
        sent.append(
            remote(x_ref.at[pl.ds(q * part, part), :], place(me, q),
                   send_own.at[q], recv_own.at[q], partner)
        )
        sent[-1].start()
    out_ref[pl.ds(pl.multiple_of(me * rows, rows), rows), :] = x_ref[...]
    passed = []
    for q in range(PIECES):
        for d in range(1, half):
            owner = lax.rem(chip - d + half, half) * 2 + core
            remote(place(owner, q), place(owner, q), send_far.at[d, q], recv_far.at[d, q], partner).wait_recv()
            passed.append(
                remote(place(owner, q), place(owner, q), send_on.at[d, q], recv_on.at[d, q], partner)
            )
            passed[-1].start()
    for copy in sent:
        copy.wait_send()
    for q in range(PIECES):
        remote(place(partner, q), place(partner, q), send_own.at[q], recv_own.at[q], partner).wait_recv()
    for copy in passed:
        copy.wait_send()
    for q in range(PIECES):
        for d in range(1, half):
            owner = lax.rem(chip - d + half, half) * 2 + 1 - core
            remote(place(owner, q), place(owner, q), send_on.at[d, q], recv_on.at[d, q], partner).wait_recv()


def gather_tokens(tokens, n):
    rows, depth = tokens.shape
    half = n // 2
    dma = pltpu.SemaphoreType.DMA
    return pl.pallas_call(
        functools.partial(gather_kernel, n),
        out_shape=jax.ShapeDtypeStruct((rows * n, depth), tokens.dtype),
        in_specs=[pl.BlockSpec(memory_space=pltpu.VMEM)],
        out_specs=pl.BlockSpec(memory_space=pltpu.VMEM),
        scratch_shapes=[dma((PIECES,)), dma((PIECES,))] + [dma((half, PIECES))] * 4,
        compiler_params=pltpu.CompilerParams(collective_id=0, has_side_effects=True),
        name="gather_tokens",
    )(tokens)


def scatter_kernel(n, p_ref, sq_ref, out_ref, total_ref, got, summed, landed, squares, s1, r1, s2, r2, s3, r3):
    me = lax.axis_index("head")
    half = n // 2
    chip, core = me // 2, me % 2
    partner = chip * 2 + 1 - core
    rows = out_ref.shape[0]
    part = rows // PIECES
    peers = [lax.rem(me + d, n) for d in range(1, n)]
    greet(peers)

    def remote(src, dst, ssem, rsem, to):
        return pltpu.make_async_remote_copy(
            src_ref=src, dst_ref=dst, send_sem=ssem, recv_sem=rsem,
            device_id={"head": to}, device_id_type=MESH,
        )

    def block(owner, q):
        return p_ref.at[pl.ds(pl.multiple_of(owner * rows + q * part, part), part), :]

    def piece(ref, d, q):
        return ref.at[d, pl.ds(q * part, part), :]

    sent = []
    for d in list(range(1, half)) + [0]:
        for q in range(PIECES):
            owner = lax.rem(chip + d, half) * 2 + 1 - core
            sent.append(remote(block(owner, q), piece(got, d, q), s1.at[d, q], r1.at[d, q], partner))
            sent[-1].start()
    for d in range(1, n):
        sent.append(remote(sq_ref.at[peers[d - 1]], squares.at[d], s3.at[d], r3.at[d], peers[d - 1]))
        sent[-1].start()
    for d in range(1, half):
        for q in range(PIECES):
            owner = lax.rem(chip + d, half) * 2 + core
            remote(piece(got, d, q), piece(got, d, q), s1.at[d, q], r1.at[d, q], partner).wait_recv()
            both = block(owner, q)[...].astype(F32) + piece(got, d, q)[...].astype(F32)
            summed[d, q * part : (q + 1) * part, :] = both.astype(BF16)
            sent.append(remote(piece(summed, d, q), piece(landed, d, q), s2.at[d, q], r2.at[d, q], owner))
            sent[-1].start()
    total = sq_ref[me]
    for d in range(1, n):
        remote(squares.at[d], squares.at[d], s3.at[d], r3.at[d], partner).wait_recv()
        total = total + squares[d]
    total_ref[...] = total
    for q in range(PIECES):
        remote(piece(got, 0, q), piece(got, 0, q), s1.at[0, q], r1.at[0, q], partner).wait_recv()
        out_ref[q * part : (q + 1) * part, :] = (
            block(me, q)[...].astype(F32) + piece(got, 0, q)[...].astype(F32)
        )
    for q in range(PIECES):
        for d in range(1, half):
            remote(piece(landed, d, q), piece(landed, d, q), s2.at[d, q], r2.at[d, q], partner).wait_recv()
            out_ref[q * part : (q + 1) * part, :] += piece(landed, d, q)[...].astype(F32)
    for copy in sent:
        copy.wait_send()


def scatter_sum(partial, squares, n):
    rows, depth = partial.shape
    rows = rows // n
    half = n // 2
    dma = pltpu.SemaphoreType.DMA
    vmem = pl.BlockSpec(memory_space=pltpu.VMEM)
    squares = jnp.broadcast_to(squares.reshape(n, 1, rows), (n, 8, rows))
    return pl.pallas_call(
        functools.partial(scatter_kernel, n),
        out_shape=[
            jax.ShapeDtypeStruct((rows, depth), F32),
            jax.ShapeDtypeStruct((8, rows), F32),
        ],
        in_specs=[vmem, vmem],
        out_specs=[vmem, vmem],
        scratch_shapes=[pltpu.VMEM((half, rows, depth), BF16)] * 3
        + [pltpu.VMEM((n, 8, rows), F32)]
        + [dma((half, PIECES))] * 4
        + [dma((n,))] * 2,
        compiler_params=pltpu.CompilerParams(collective_id=1, has_side_effects=True),
        name="scatter_sum",
    )(partial, squares)


def chain_kernel(
    n_seq, width, packed_ref, rows_ref, wz_ref, x_ref, step_ref, cum_ref, cumt_ref, b_ref, c_ref,
    skip_ref, gain_ref, out_ref, sq_ref, y_ref, z_ref, held, came, send_sem, recv_sem,
):
    me = lax.axis_index("seq")
    n = b_ref.shape[1]
    blocks, _, hb = step_ref.shape
    wide = hb * width
    steps = [1]
    while 2 * steps[-1] < n_seq:
        steps.append(2 * steps[-1])
    if len(steps) == 1:
        steps.append(2)
    barrier = pltpu.get_barrier_semaphore()
    for d in steps:
        for peer in (lax.rem(me + d, n_seq), lax.rem(me - d + n_seq, n_seq)):
            pl.semaphore_signal(barrier, inc=1, device_id={"seq": peer}, device_id_type=MESH)
    pl.semaphore_wait(barrier, 2 * len(steps))

    def z_unit(j):
        z_ref[:, j * wide : (j + 1) * wide] = jnp.dot(
            rows_ref[...], wz_ref[:, j * wide : (j + 1) * wide], preferred_element_type=F32
        )

    def local_unit(j):
        at = pl.ds(j * wide, wide)
        one = pl.ds(j, 1)
        local_kernel(
            width, x_ref.at[:, at], step_ref.at[one], cum_ref.at[one], cumt_ref.at[one],
            b_ref, c_ref, skip_ref.at[one], y_ref.at[:, at],
        )

    units = [functools.partial(f, j) for j in range(blocks) for f in (local_unit, z_unit)]
    distances = [1, 2] + steps[1:]
    last = len(distances)
    cuts = [0] + [(k + 1) * len(units) // (last - 1) for k in range(last - 1)]

    def copy_of(k, d):
        return pltpu.make_async_remote_copy(
            src_ref=packed_ref if k < 2 else held.at[k],
            dst_ref=came.at[k], send_sem=send_sem.at[k], recv_sem=recv_sem.at[k],
            device_id={"seq": lax.rem(me + d, n_seq)}, device_id_type=MESH,
        )

    def start(k):
        d = distances[k]

        @pl.when(me + d < n_seq)
        def _():
            copy_of(k, d).start()

    def combine(k):
        d = distances[k]

        @pl.when(me >= d)
        def _():
            copy_of(k, d).wait_recv()
            for j in range(blocks):
                at = slice(j * wide, (j + 1) * wide)
                earlier = came[k, :, at].astype(F32)
                if k > 0:
                    mine = held[k, :, at].astype(F32)
                    decay = mine[n : n + 1]
                    earlier = jnp.concatenate([decay * earlier[:n] + mine[:n], decay * earlier[n:]], axis=0)
                held[k + 1, :, at] = earlier.astype(BF16)

        @pl.when(me < d)
        def _():
            held[k + 1] = jnp.zeros_like(held[k + 1]) if k == 0 else held[k]

        @pl.when(me + d < n_seq)
        def _():
            copy_of(k, d).wait_send()

    start(0)
    start(1)
    for phase in range(last - 1):
        for unit in units[cuts[phase] : cuts[phase + 1]]:
            unit()
        if phase == 0:
            combine(0)
        combine(phase + 1)
        if phase + 2 < last:
            start(phase + 2)
    sq_ref[...] = jnp.zeros_like(sq_ref)
    entering = held.at[last]
    for j in range(blocks):
        at = pl.ds(j * wide, wide)
        gate_block(
            width, y_ref.at[:, at], z_ref.at[:, at], cum_ref.at[pl.ds(j, 1)], c_ref,
            entering.at[pl.ds(0, n), at], gain_ref.at[:, at], out_ref.at[:, at], sq_ref,
        )


def per_device(
    tokens, w_in_x, w_in_z, w_in_bc, w_dt, conv_x, conv_bc, dt_bias, decay_rate, skip, norm_gain, w_out
):
    cols = w_in_x.shape[1]
    heads = dt_bias.shape[0]
    width = cols // heads
    n = w_in_bc.shape[1] // 2
    inner = cols * lax.axis_size("head")
    rows_all = gather_tokens(tokens, lax.axis_size("head"))
    rows = rows_all.shape[0]
    dot = functools.partial(jnp.dot, preferred_element_type=F32)
    x_proj = dot(rows_all, w_in_x)
    small = dot(rows_all, jnp.concatenate([w_in_bc, w_dt], axis=1))
    bc_proj, step_raw = small[:, : 2 * n], small[:, 2 * n :]
    before = passed_along(
        jnp.concatenate([x_proj[-8:], bc_proj[-8:]], axis=1), "seq", 1
    )
    x_before, bc_before = before[:, :cols], before[:, cols:]
    padded = jnp.concatenate([bc_before, bc_proj], axis=0)
    bc = sum(conv_bc[k] * padded[5 + k : 5 + k + rows] for k in range(KERNEL))
    bc = jax.nn.silu(bc).astype(BF16)
    b_mat, c_mat = bc[:, :n], bc[:, n:]
    step = jax.nn.softplus(step_raw + dt_bias)
    order = jnp.arange(rows)
    tri = (order[:, None] >= order[None, :]).astype(F32)
    cumul = jnp.dot(tri, -step * decay_rate, precision=highest)
    total = cumul[-1:]

    hb = min(heads, 256 // width)
    blocks = heads // hb
    wide = hb * width

    def by_block(a):
        return a.reshape(a.shape[0], blocks, hb).transpose(1, 0, 2)

    total3 = by_block(total)
    full = lambda r: pl.BlockSpec((r, wide), lambda j: (0, j))
    same = lambda r, c: pl.BlockSpec((r, c), lambda j: (0, 0))
    lead = lambda r, c: pl.BlockSpec((1, r, c), lambda j: (j, 0, 0))
    x_conv, packed = pl.pallas_call(
        functools.partial(conv_state_kernel, width),
        grid=(blocks,),
        in_specs=[full(rows), full(8), full(KERNEL), lead(rows, hb), lead(1, hb), same(rows, n)],
        out_specs=[full(rows), full(n + 16)],
        out_shape=[
            jax.ShapeDtypeStruct((rows, cols), F32),
            jax.ShapeDtypeStruct((n + 16, cols), BF16),
        ],
        scratch_shapes=[pltpu.VMEM((rows + 8, wide), F32)],
        cost_estimate=pl.CostEstimate(
            flops=2 * rows * n * cols, bytes_accessed=8 * rows * cols, transcendentals=rows * cols
        ),
        name="conv_state",
    )(x_proj, x_before, conv_x, by_block(step * jnp.exp(total - cumul)), total3, b_mat)

    n_seq = lax.axis_size("seq")
    stages = 1 + max(2, (n_seq - 1).bit_length())
    vmem = pl.BlockSpec(memory_space=pltpu.VMEM)
    gated, squares = pl.pallas_call(
        functools.partial(chain_kernel, n_seq, width),
        out_shape=[
            jax.ShapeDtypeStruct((rows, cols), BF16),
            jax.ShapeDtypeStruct((rows, 1), F32),
        ],
        in_specs=[vmem] * 11,
        out_specs=[vmem, vmem],
        scratch_shapes=[
            pltpu.VMEM((rows, cols), F32),
            pltpu.VMEM((rows, cols), F32),
            pltpu.VMEM((stages + 1, n + 16, cols), BF16),
            pltpu.VMEM((stages, n + 16, cols), BF16),
            pltpu.SemaphoreType.DMA((stages,)),
            pltpu.SemaphoreType.DMA((stages,)),
        ],
        compiler_params=pltpu.CompilerParams(collective_id=2, has_side_effects=True),
        name="state_chain",
    )(
        packed, rows_all, w_in_z, x_conv, by_block(step), by_block(cumul),
        cumul.T.reshape(blocks, hb, rows), b_mat, c_mat, by_block(skip[None, :]), norm_gain[None, :],
    )
    mixed, squares = scatter_sum(dot(gated, w_out).astype(BF16), squares[:, 0], lax.axis_size("head"))
    scale = lax.rsqrt(squares[0] / inner + 1e-05)
    return (mixed * scale[:, None]).astype(BF16)


def solution(mesh):
    placed = (
        P(("seq", "head"), None), P(None, "head"), P(None, "head"), P(), P(None, "head"),
        P(None, "head"), P(), P("head"), P("head"), P("head"), P("head"), P("head", None),
    )
    return jax.shard_map(
        per_device, mesh=mesh, in_specs=placed, out_specs=P(("seq", "head"), None), check_vma=False
    )
```

```python
import functools
import jax
import jax.numpy as jnp
from jax import lax
from jax.experimental import pallas as pl
from jax.experimental.pallas import tpu as pltpu
from jax.sharding import PartitionSpec as P

CHUNK = 128
KERNEL = 4
F32 = jnp.float32
BF16 = jnp.bfloat16
highest = lax.Precision.HIGHEST


def passed_along(block, axis, distance):
    devices = range(lax.axis_size(axis))
    route = [(i - distance, i) for i in devices if i - distance in devices]
    return lax.ppermute(block, axis, route)


def widen(columns, width):
    rows, heads = columns.shape
    lane = lax.broadcasted_iota(jnp.int32, (rows, 2 * width), 1)
    parts = []
    for h in range(0, heads, 2):
        left = jnp.broadcast_to(columns[:, h : h + 1], (rows, 2 * width))
        right = jnp.broadcast_to(columns[:, h + 1 : h + 2], (rows, 2 * width))
        parts.append(jnp.where(lane < width, left, right))
    return jnp.concatenate(parts, axis=1)


def conv_state_kernel(width, x_ref, before_ref, taps_ref, weight_ref, total_ref, b_ref, conv_ref, state_ref, pad_ref):
    rows = x_ref.shape[0]
    pad_ref[0:8, :] = before_ref[...]
    pad_ref[8 : 8 + rows, :] = x_ref[...]
    for r in range(0, rows, CHUNK):
        acc = taps_ref[0:1, :] * pad_ref[r + 5 : r + 5 + CHUNK, :]
        for k in range(1, KERNEL):
            acc = acc + taps_ref[k : k + 1, :] * pad_ref[r + 5 + k : r + 5 + k + CHUNK, :]
        value = acc / (1.0 + jnp.exp(-acc))
        conv_ref[r : r + CHUNK, :] = value
        fresh = (value * widen(weight_ref[0, r : r + CHUNK, :], width)).astype(BF16)
        part = lax.dot_general(
            b_ref[r : r + CHUNK, :], fresh, (((0,), (0,)), ((), ())), preferred_element_type=F32
        )
        state = part if r == 0 else state + part
    n = state.shape[0]
    state_ref[0:n, :] = state.astype(BF16)
    decay = jnp.broadcast_to(jnp.exp(total_ref[0]), (16, total_ref.shape[2]))
    state_ref[n : n + 16, :] = widen(decay, width).astype(BF16)


def local_kernel(width, x_ref, step_ref, cum_ref, cumt_ref, b_ref, c_ref, skip_ref, y_ref):
    rows, cols = x_ref.shape
    heads = cols // width
    t = lax.broadcasted_iota(jnp.int32, (CHUNK, CHUNK), 0)
    s = lax.broadcasted_iota(jnp.int32, (CHUNK, CHUNK), 1)
    lower = t >= s
    lane = lax.broadcasted_iota(jnp.int32, (CHUNK, 2 * width), 1)
    skip = widen(jnp.broadcast_to(skip_ref[0], (8, heads)), width)[0:1, :]
    state = None
    base = jnp.zeros((1, heads), F32)
    for r in range(0, rows, CHUNK):
        x = x_ref[r : r + CHUNK, :]
        b = b_ref[r : r + CHUNK, :]
        c = c_ref[r : r + CHUNK, :]
        cum = cum_ref[0, r : r + CHUNK, :]
        scaled = x * widen(step_ref[0, r : r + CHUNK, :], width)
        narrow = scaled.astype(BF16)
        scores = lax.dot_general(c, b, (((1,), (1,)), ((), ())), preferred_element_type=F32)
        scores = jnp.where(lower, scores, 0.0)
        pieces = []
        for h in range(0, heads, 2):
            pair = narrow[:, h * width : (h + 2) * width]
            both = []
            for g in (h, h + 1):
                spread = cum[:, g : g + 1] - cumt_ref[0, g : g + 1, r : r + CHUNK]
                within = scores * jnp.exp(jnp.minimum(spread, 0.0))
                both.append(jnp.dot(within.astype(BF16), pair, preferred_element_type=F32))
            pieces.append(jnp.where(lane < width, both[0], both[1]))
        y = jnp.concatenate(pieces, axis=1) + skip * x
        last = cum_ref[0, r + CHUNK - 1 : r + CHUNK, :]
        if state is not None:
            y = y + jnp.dot(c, state.astype(BF16), preferred_element_type=F32) * widen(
                jnp.exp(cum - base), width
            )
        y_ref[r : r + CHUNK, :] = y
        if r + CHUNK < rows:
            rest = (scaled * widen(jnp.exp(last - cum), width)).astype(BF16)
            fresh = lax.dot_general(b, rest, (((0,), (0,)), ((), ())), preferred_element_type=F32)
            if state is None:
                state = fresh
            else:
                kept = widen(jnp.broadcast_to(jnp.exp(last - base), (8, heads)), width)[0:1, :]
                state = kept * state + fresh
            base = last


def gate_block(width, y_ref, z_ref, cum_ref, c_ref, state_ref, gain_ref, out_ref, sq_ref):
    for r in range(0, y_ref.shape[0], CHUNK):
        at = slice(r, r + CHUNK)
        carried = jnp.dot(c_ref[at, :], state_ref[...], preferred_element_type=F32)
        ssd = y_ref[at, :] + carried * widen(jnp.exp(cum_ref[0, at, :]), width)
        z = z_ref[at, :]
        gated = ssd * (z / (1.0 + jnp.exp(-z)))
        sq_ref[at, :] += jnp.sum(gated * gated, axis=1, keepdims=True)
        out_ref[at, :] = (gated * gain_ref[...]).astype(BF16)


MESH = pl.DeviceIdType.MESH
PIECES = 8


def greet(peers):
    barrier = pltpu.get_barrier_semaphore()
    for peer in peers:
        pl.semaphore_signal(barrier, inc=1, device_id={"head": peer}, device_id_type=MESH)
    pl.semaphore_wait(barrier, len(peers))


def gather_kernel(n, x_ref, out_ref, send_own, recv_own, send_far, recv_far, send_on, recv_on):
    me = lax.axis_index("head")
    half = n // 2
    chip, core = me // 2, me % 2
    partner = chip * 2 + 1 - core
    rows = x_ref.shape[0]
    part = rows // PIECES
    far = [lax.rem(chip + d, half) * 2 + core for d in range(1, half)]
    greet([partner] + far)

    def remote(src, dst, ssem, rsem, to):
        return pltpu.make_async_remote_copy(
            src_ref=src, dst_ref=dst, send_sem=ssem, recv_sem=rsem,
            device_id={"head": to}, device_id_type=MESH,
        )

    def place(owner, q):
        return out_ref.at[pl.ds(pl.multiple_of(owner * rows + q * part, part), part), :]

    sent = []
    for q in range(PIECES):
        for d in range(1, half):
            sent.append(
                remote(x_ref.at[pl.ds(q * part, part), :], place(me, q),
                       send_far.at[d, q], recv_far.at[d, q], far[d - 1])
            )
            sent[-1].start()
    for q in range(PIECES):
        sent.append(
            remote(x_ref.at[pl.ds(q * part, part), :], place(me, q),
                   send_own.at[q], recv_own.at[q], partner)
        )
        sent[-1].start()
    out_ref[pl.ds(pl.multiple_of(me * rows, rows), rows), :] = x_ref[...]
    passed = []
    for q in range(PIECES):
        for d in range(1, half):
            owner = lax.rem(chip - d + half, half) * 2 + core
            remote(place(owner, q), place(owner, q), send_far.at[d, q], recv_far.at[d, q], partner).wait_recv()
            passed.append(
                remote(place(owner, q), place(owner, q), send_on.at[d, q], recv_on.at[d, q], partner)
            )
            passed[-1].start()
    for copy in sent:
        copy.wait_send()
    for q in range(PIECES):
        remote(place(partner, q), place(partner, q), send_own.at[q], recv_own.at[q], partner).wait_recv()
    for copy in passed:
        copy.wait_send()
    for q in range(PIECES):
        for d in range(1, half):
            owner = lax.rem(chip - d + half, half) * 2 + 1 - core
            remote(place(owner, q), place(owner, q), send_on.at[d, q], recv_on.at[d, q], partner).wait_recv()


def gather_tokens(tokens, n):
    rows, depth = tokens.shape
    half = n // 2
    dma = pltpu.SemaphoreType.DMA
    return pl.pallas_call(
        functools.partial(gather_kernel, n),
        out_shape=jax.ShapeDtypeStruct((rows * n, depth), tokens.dtype),
        in_specs=[pl.BlockSpec(memory_space=pltpu.VMEM)],
        out_specs=pl.BlockSpec(memory_space=pltpu.VMEM),
        scratch_shapes=[dma((PIECES,)), dma((PIECES,))] + [dma((half, PIECES))] * 4,
        compiler_params=pltpu.CompilerParams(collective_id=0, has_side_effects=True),
        name="gather_tokens",
    )(tokens)


def scatter_kernel(n, p_ref, sq_ref, out_ref, total_ref, got, summed, landed, squares, s1, r1, s2, r2, s3, r3):
    me = lax.axis_index("head")
    half = n // 2
    chip, core = me // 2, me % 2
    partner = chip * 2 + 1 - core
    rows = out_ref.shape[0]
    part = rows // PIECES
    peers = [lax.rem(me + d, n) for d in range(1, n)]
    greet(peers)

    def remote(src, dst, ssem, rsem, to):
        return pltpu.make_async_remote_copy(
            src_ref=src, dst_ref=dst, send_sem=ssem, recv_sem=rsem,
            device_id={"head": to}, device_id_type=MESH,
        )

    def block(owner, q):
        return p_ref.at[pl.ds(pl.multiple_of(owner * rows + q * part, part), part), :]

    def piece(ref, d, q):
        return ref.at[d, pl.ds(q * part, part), :]

    sent = []
    for d in list(range(1, half)) + [0]:
        for q in range(PIECES):
            owner = lax.rem(chip + d, half) * 2 + 1 - core
            sent.append(remote(block(owner, q), piece(got, d, q), s1.at[d, q], r1.at[d, q], partner))
            sent[-1].start()
    for d in range(1, n):
        sent.append(remote(sq_ref.at[peers[d - 1]], squares.at[d], s3.at[d], r3.at[d], peers[d - 1]))
        sent[-1].start()
    for d in range(1, half):
        for q in range(PIECES):
            owner = lax.rem(chip + d, half) * 2 + core
            remote(piece(got, d, q), piece(got, d, q), s1.at[d, q], r1.at[d, q], partner).wait_recv()
            both = block(owner, q)[...].astype(F32) + piece(got, d, q)[...].astype(F32)
            summed[d, q * part : (q + 1) * part, :] = both.astype(BF16)
            sent.append(remote(piece(summed, d, q), piece(landed, d, q), s2.at[d, q], r2.at[d, q], owner))
            sent[-1].start()
    total = sq_ref[me]
    for d in range(1, n):
        remote(squares.at[d], squares.at[d], s3.at[d], r3.at[d], partner).wait_recv()
        total = total + squares[d]
    total_ref[...] = total
    for q in range(PIECES):
        remote(piece(got, 0, q), piece(got, 0, q), s1.at[0, q], r1.at[0, q], partner).wait_recv()
        out_ref[q * part : (q + 1) * part, :] = (
            block(me, q)[...].astype(F32) + piece(got, 0, q)[...].astype(F32)
        )
    for q in range(PIECES):
        for d in range(1, half):
            remote(piece(landed, d, q), piece(landed, d, q), s2.at[d, q], r2.at[d, q], partner).wait_recv()
            out_ref[q * part : (q + 1) * part, :] += piece(landed, d, q)[...].astype(F32)
    for copy in sent:
        copy.wait_send()


def scatter_sum(partial, squares, n):
    rows, depth = partial.shape
    rows = rows // n
    half = n // 2
    dma = pltpu.SemaphoreType.DMA
    vmem = pl.BlockSpec(memory_space=pltpu.VMEM)
    squares = jnp.broadcast_to(squares.reshape(n, 1, rows), (n, 8, rows))
    return pl.pallas_call(
        functools.partial(scatter_kernel, n),
        out_shape=[
            jax.ShapeDtypeStruct((rows, depth), F32),
            jax.ShapeDtypeStruct((8, rows), F32),
        ],
        in_specs=[vmem, vmem],
        out_specs=[vmem, vmem],
        scratch_shapes=[pltpu.VMEM((half, rows, depth), BF16)] * 3
        + [pltpu.VMEM((n, 8, rows), F32)]
        + [dma((half, PIECES))] * 4
        + [dma((n,))] * 2,
        compiler_params=pltpu.CompilerParams(collective_id=1, has_side_effects=True),
        name="scatter_sum",
    )(partial, squares)


def chain_kernel(
    n_seq, width, packed_ref, rows_ref, wz_ref, x_ref, step_ref, cum_ref, cumt_ref, b_ref, c_ref,
    skip_ref, gain_ref, out_ref, sq_ref, y_ref, z_ref, held, came, send_sem, recv_sem,
):
    me = lax.axis_index("seq")
    n = b_ref.shape[1]
    blocks, _, hb = step_ref.shape
    wide = hb * width
    steps = [1]
    while 2 * steps[-1] < n_seq:
        steps.append(2 * steps[-1])
    if len(steps) == 1:
        steps.append(2)
    barrier = pltpu.get_barrier_semaphore()
    for d in steps:
        for peer in (lax.rem(me + d, n_seq), lax.rem(me - d + n_seq, n_seq)):
            pl.semaphore_signal(barrier, inc=1, device_id={"seq": peer}, device_id_type=MESH)
    pl.semaphore_wait(barrier, 2 * len(steps))

    def z_unit(j):
        z_ref[:, j * wide : (j + 1) * wide] = jnp.dot(
            rows_ref[...], wz_ref[:, j * wide : (j + 1) * wide], preferred_element_type=F32
        )

    def local_unit(j):
        at = pl.ds(j * wide, wide)
        one = pl.ds(j, 1)
        local_kernel(
            width, x_ref.at[:, at], step_ref.at[one], cum_ref.at[one], cumt_ref.at[one],
            b_ref, c_ref, skip_ref.at[one], y_ref.at[:, at],
        )

    units = [functools.partial(f, j) for j in range(blocks) for f in (local_unit, z_unit)]
    distances = [1, 2] + steps[1:]
    last = len(distances)
    cuts = [0] + [(k + 1) * len(units) // (last - 1) for k in range(last - 1)]

    def copy_of(k, d):
        return pltpu.make_async_remote_copy(
            src_ref=packed_ref if k < 2 else held.at[k],
            dst_ref=came.at[k], send_sem=send_sem.at[k], recv_sem=recv_sem.at[k],
            device_id={"seq": lax.rem(me + d, n_seq)}, device_id_type=MESH,
        )

    def start(k):
        d = distances[k]

        @pl.when(me + d < n_seq)
        def _():
            copy_of(k, d).start()

    def combine(k):
        d = distances[k]

        @pl.when(me >= d)
        def _():
            copy_of(k, d).wait_recv()
            for j in range(blocks):
                at = slice(j * wide, (j + 1) * wide)
                earlier = came[k, :, at].astype(F32)
                if k > 0:
                    mine = held[k, :, at].astype(F32)
                    decay = mine[n : n + 1]
                    earlier = jnp.concatenate([decay * earlier[:n] + mine[:n], decay * earlier[n:]], axis=0)
                held[k + 1, :, at] = earlier.astype(BF16)

        @pl.when(me < d)
        def _():
            held[k + 1] = jnp.zeros_like(held[k + 1]) if k == 0 else held[k]

        @pl.when(me + d < n_seq)
        def _():
            copy_of(k, d).wait_send()

    start(0)
    start(1)
    for phase in range(last - 1):
        for unit in units[cuts[phase] : cuts[phase + 1]]:
            unit()
        if phase == 0:
            combine(0)
        combine(phase + 1)
        if phase + 2 < last:
            start(phase + 2)
    sq_ref[...] = jnp.zeros_like(sq_ref)
    entering = held.at[last]
    for j in range(blocks):
        at = pl.ds(j * wide, wide)
        gate_block(
            width, y_ref.at[:, at], z_ref.at[:, at], cum_ref.at[pl.ds(j, 1)], c_ref,
            entering.at[pl.ds(0, n), at], gain_ref.at[:, at], out_ref.at[:, at], sq_ref,
        )


def per_device(
    tokens, w_in_x, w_in_z, w_in_bc, w_dt, conv_x, conv_bc, dt_bias, decay_rate, skip, norm_gain, w_out
):
    cols = w_in_x.shape[1]
    heads = dt_bias.shape[0]
    width = cols // heads
    n = w_in_bc.shape[1] // 2
    inner = cols * lax.axis_size("head")
    rows_all = gather_tokens(tokens, lax.axis_size("head"))
    rows = rows_all.shape[0]
    dot = functools.partial(jnp.dot, preferred_element_type=F32)
    x_proj = dot(rows_all, w_in_x)
    small = dot(rows_all, jnp.concatenate([w_in_bc, w_dt], axis=1))
    bc_proj, step_raw = small[:, : 2 * n], small[:, 2 * n :]
    before = passed_along(
        jnp.concatenate([x_proj[-8:], bc_proj[-8:]], axis=1), "seq", 1
    )
    x_before, bc_before = before[:, :cols], before[:, cols:]
    padded = jnp.concatenate([bc_before, bc_proj], axis=0)
    bc = sum(conv_bc[k] * padded[5 + k : 5 + k + rows] for k in range(KERNEL))
    bc = jax.nn.silu(bc).astype(BF16)
    b_mat, c_mat = bc[:, :n], bc[:, n:]
    step = jax.nn.softplus(step_raw + dt_bias)
    order = jnp.arange(rows)
    tri = (order[:, None] >= order[None, :]).astype(F32)
    cumul = jnp.dot(tri, -step * decay_rate, precision=highest)
    total = cumul[-1:]

    hb = min(heads, 256 // width)
    blocks = heads // hb
    wide = hb * width

    def by_block(a):
        return a.reshape(a.shape[0], blocks, hb).transpose(1, 0, 2)

    total3 = by_block(total)
    full = lambda r: pl.BlockSpec((r, wide), lambda j: (0, j))
    same = lambda r, c: pl.BlockSpec((r, c), lambda j: (0, 0))
    lead = lambda r, c: pl.BlockSpec((1, r, c), lambda j: (j, 0, 0))
    x_conv, packed = pl.pallas_call(
        functools.partial(conv_state_kernel, width),
        grid=(blocks,),
        in_specs=[full(rows), full(8), full(KERNEL), lead(rows, hb), lead(1, hb), same(rows, n)],
        out_specs=[full(rows), full(n + 16)],
        out_shape=[
            jax.ShapeDtypeStruct((rows, cols), F32),
            jax.ShapeDtypeStruct((n + 16, cols), BF16),
        ],
        scratch_shapes=[pltpu.VMEM((rows + 8, wide), F32)],
        cost_estimate=pl.CostEstimate(
            flops=2 * rows * n * cols, bytes_accessed=8 * rows * cols, transcendentals=rows * cols
        ),
        name="conv_state",
    )(x_proj, x_before, conv_x, by_block(step * jnp.exp(total - cumul)), total3, b_mat)

    n_seq = lax.axis_size("seq")
    stages = 1 + max(2, (n_seq - 1).bit_length())
    vmem = pl.BlockSpec(memory_space=pltpu.VMEM)
    gated, squares = pl.pallas_call(
        functools.partial(chain_kernel, n_seq, width),
        out_shape=[
            jax.ShapeDtypeStruct((rows, cols), BF16),
            jax.ShapeDtypeStruct((rows, 1), F32),
        ],
        in_specs=[vmem] * 11,
        out_specs=[vmem, vmem],
        scratch_shapes=[
            pltpu.VMEM((rows, cols), F32),
            pltpu.VMEM((rows, cols), F32),
            pltpu.VMEM((stages + 1, n + 16, cols), BF16),
            pltpu.VMEM((stages, n + 16, cols), BF16),
            pltpu.SemaphoreType.DMA((stages,)),
            pltpu.SemaphoreType.DMA((stages,)),
        ],
        compiler_params=pltpu.CompilerParams(collective_id=2, has_side_effects=True),
        name="state_chain",
    )(
        packed, rows_all, w_in_z, x_conv, by_block(step), by_block(cumul),
        cumul.T.reshape(blocks, hb, rows), b_mat, c_mat, by_block(skip[None, :]), norm_gain[None, :],
    )
    mixed, squares = scatter_sum(dot(gated, w_out).astype(BF16), squares[:, 0], lax.axis_size("head"))
    scale = lax.rsqrt(squares[0] / inner + 1e-05)
    return (mixed * scale[:, None]).astype(BF16)


def solution(mesh):
    placed = (
        P(("seq", "head"), None), P(None, "head"), P(None, "head"), P(), P(None, "head"),
        P(None, "head"), P(), P("head"), P("head"), P("head"), P("head"), P("head", None),
    )
    return jax.shard_map(
        per_device, mesh=mesh, in_specs=placed, out_specs=P(("seq", "head"), None), check_vma=False
    )
```
